32 devices in a mesh: fsdp: 16 (over z, y, x), rep: 2 (over core).
Axes of the slice: x: 2, y: 2, z: 4, core: 2. Of those that a mesh axis runs over, the one named last changes fastest.
Arguments:
- tokens: bfloat16 [4096, 1024], P(('fsdp', 'rep')), may hold values from -6 to 6
- segment_ids: int32 [64, 64], P(('fsdp', 'rep')), may hold values from 0 to 2, as said below
- w_qkv: bfloat16 [1024, 3072], P('fsdp'), as said below
- qv_bias: bfloat16 [2048], P('fsdp'), may hold values from -3 to 3
- w_out: bfloat16 [1024, 1024], P('fsdp'), may hold values from -0.75 to 0.75
- ln1_gain: bfloat16 [1024], P('fsdp'), may hold values from 0.5 to 1.5
- ln1_bias: bfloat16 [1024], P('fsdp'), may hold values from -3 to 3
- w_gate: bfloat16 [1024, 2816], P('fsdp'), may hold values from -0.1875 to 0.1875
- w_up: bfloat16 [1024, 2816], P('fsdp'), may hold values from -0.1875 to 0.1875
- w_down: bfloat16 [2816, 1024], P('fsdp'), may hold values from -0.21875 to 0.21875
- ln2_gain: bfloat16 [1024], P('fsdp'), may hold values from 0.5 to 1.5
- ln2_bias: bfloat16 [1024], P('fsdp'), may hold values from -3 to 3
- out_grad: bfloat16 [4096, 1024], P(('fsdp', 'rep')), may hold values from -6 to 6
Outputs:
- result: bfloat16 [4096, 1024], P(('fsdp', 'rep'))
- grad_tokens: bfloat16 [4096, 1024], P(('fsdp', 'rep'))
- grad_w_qkv: float32 [1024, 3072], P('fsdp')
- grad_qv_bias: float32 [2048], P('fsdp')
- grad_w_out: float32 [1024, 1024], P('fsdp')
- grad_ln1_gain: float32 [1024], P('fsdp')
- grad_ln1_bias: float32 [1024], P('fsdp')
- grad_w_gate: float32 [1024, 2816], P('fsdp')
- grad_w_up: float32 [1024, 2816], P('fsdp')
- grad_w_down: float32 [2816, 1024], P('fsdp')
- grad_ln2_gain: float32 [1024], P('fsdp')
- grad_ln2_bias: float32 [1024], P('fsdp')
The draws below stay inside these ranges and needn't reach their ends.
Inputs may be any that keep to these rules, and one draw needn't show every extreme that they name: `segment_ids`: within each micro-batch the ids start at 0, never fall and rise by one at a time, so each of the 3 sequences fills a run of slots. `w_qkv`: no structure is promised.
All inputs are finite; a program needn't handle non-finite values.
Results may differ from the reference program's by a relative error of at most 0.012.
Values may be sent and summed in bfloat16 or wider, within the bound.
No kernel may reach another device: no remote copies, remote signals or barrier semaphores. Data moves between devices by JAX's collectives and lax.ppermute only.
A program may use at most 192 MiB of HBM per device.

```python
import jax
import jax.numpy as jnp
from jax import lax

D = 1024
H = 16
HD = 64
FF = 2816
ROT = 16
CAP = 64
MB = 2
NSEG = 3
MBATCH = 64
TOKENS = 4096


def draw_segment_ids(key, part):
    scores = jax.random.randint(key, (MBATCH, CAP - 1), 0, 1 << 20) * CAP + jnp.arange(CAP - 1, dtype=jnp.int32)
    picked = lax.top_k(scores, NSEG - 1)[1] + 1
    order = jnp.arange(CAP, dtype=jnp.int32)
    return jnp.sum((order[None, :, None] >= picked[:, None, :]).astype(jnp.int32), axis=-1)


def draw_w_qkv(key, part):
    base = jax.random.normal(key, (D, 3 * D), jnp.float32) * D ** (-0.5)
    return base.astype(jnp.bfloat16)


def level_of(key, extent, shards, least, largest):
    level, own = 1.0, jax.random.fold_in(key, 6)
    for position, shards_of in shards:
        heights = jnp.exp(jax.random.uniform(jax.random.fold_in(own, position), (shards_of,), jnp.float32, least / len(shards), largest / len(shards)))
        level = level * jnp.repeat(heights, extent[position] // shards_of).reshape([-1 if axis == position else 1 for axis in range(len(extent))])
    return level


def normal_values(stream_key, shape, spread, reach, shards=(), held_as=jnp.bfloat16):
    values = jax.random.normal(stream_key, shape, jnp.float32) * spread
    if len(shards) > 0:
        values = level_of(stream_key, shape, shards, -0.22, 0.18) * values
    return jnp.clip(values, min=-reach, max=reach).astype(held_as)


def setup_inputs(seed: int = 0) -> dict:
    streams_of = jax.random.split(jax.random.key(seed), 14)
    return {
        "tokens": normal_values(streams_of[0], (TOKENS, D), 1.0, 6.0, ((0, 32),)),
        "segment_ids": draw_segment_ids(jax.random.fold_in(streams_of[13], 71), 0),
        "w_qkv": draw_w_qkv(jax.random.fold_in(streams_of[13], 71), 0),
        "qv_bias": normal_values(streams_of[3], (2 * D,), 0.5, 3.0, ((0, 16),)),
        "w_out": normal_values(streams_of[4], (D, D), (D // 16) ** -0.5, 0.75, ((0, 16),)),
        "ln1_gain": jnp.clip(0.5 + 1.0 * jax.random.uniform(streams_of[5], (D,), jnp.float32) ** level_of(streams_of[5], (D,), ((0, 16),), -0.2, 0.2), 0.5, 1.5).astype(jnp.bfloat16),
        "ln1_bias": normal_values(streams_of[6], (D,), 0.5, 3.0, ((0, 16),)),
        "w_gate": normal_values(streams_of[7], (D, FF), D ** -0.5, 0.1875, ((0, 16),)),
        "w_up": normal_values(streams_of[8], (D, FF), D ** -0.5, 0.1875, ((0, 16),)),
        "w_down": normal_values(streams_of[9], (FF, D), (FF // 4) ** -0.5, 0.21875, ((0, 16),)),
        "ln2_gain": jnp.clip(0.5 + 1.0 * jax.random.uniform(streams_of[10], (D,), jnp.float32) ** level_of(streams_of[10], (D,), ((0, 16),), -0.2, 0.2), 0.5, 1.5).astype(jnp.bfloat16),
        "ln2_bias": normal_values(streams_of[11], (D,), 0.5, 3.0, ((0, 16),)),
        "out_grad": normal_values(streams_of[12], (TOKENS, D), 1.0, 6.0, ((0, 32),)),
    }


EPS = 1e-05
HIGHEST = lax.Precision.HIGHEST

@jax.custom_vjp
def low(v):
    return lax.optimization_barrier(v.astype(jnp.bfloat16)).astype(jnp.float32)

@jax.custom_vjp
def low_back(v):
    return v

def low_keep(v):
    return (low(v), None)

def low_pass(kept, grad):
    return (grad,)

def back_keep(v):
    return (v, None)

def back_low(kept, grad):
    return (low(grad),)
low.defvjp(low_keep, low_pass)
low_back.defvjp(back_keep, back_low)

def layer_norm(values, gain, shift):
    center = lax.optimization_barrier(jnp.mean(values, axis=-1, keepdims=True))
    shifted = values - center
    variance = lax.optimization_barrier(jnp.mean(shifted * shifted, axis=-1, keepdims=True))
    return shifted * lax.rsqrt(variance + EPS) * gain + shift

def slot_layout(segments):
    width = segments.shape[1]
    same = segments[:, :, None] == segments[:, None, :]
    order = jnp.arange(width)
    earlier = order[:, None] > order[None, :]
    positions = lax.optimization_barrier(jnp.sum((same & earlier).astype(jnp.float32), axis=-1))
    allowed = same & (order[:, None] >= order[None, :])
    return (positions, allowed)

def rotary_tables(positions):
    freqs = 10000.0 ** (-2.0 * jnp.arange(ROT // 2, dtype=jnp.float32) / ROT)
    angles = positions[:, :, None, None] * freqs
    return (jnp.cos(angles), jnp.sin(angles))

def rotate(values, cosine, sine):
    half = ROT // 2
    first = values[..., :half]
    second = values[..., half:ROT]
    return jnp.concatenate([first * cosine - second * sine, second * cosine + first * sine, values[..., ROT:]], axis=-1)

def forward(inputs, segments, w_qkv, qv_bias, w_out, gain_one, shift_one, w_gate, w_up, w_down, gain_two, shift_two):
    batches = segments.shape[0]
    rows = inputs.shape[0]
    positions, allowed = slot_layout(segments)
    cosine, sine = rotary_tables(positions)
    hidden_one = low(layer_norm(inputs, gain_one, shift_one))
    bias_row = jnp.concatenate([qv_bias[:D], jnp.zeros((D,), jnp.float32), qv_bias[D:]])
    projected = low_back(jnp.dot(hidden_one, w_qkv, precision=HIGHEST) + bias_row)
    projected = projected.reshape(batches, CAP, 3, H, HD)
    queries = low(rotate(projected[:, :, 0], cosine, sine))
    keys = low(rotate(projected[:, :, 1], cosine, sine))
    values = low(projected[:, :, 2])
    scores = low_back(jnp.einsum('bqhd,bkhd->bhqk', queries, keys, precision=HIGHEST) * 0.125)
    scores = jnp.where(allowed[:, None], scores, -1e+30)
    highest = lax.optimization_barrier(jnp.max(scores, axis=-1, keepdims=True))
    raised = jnp.exp(scores - highest)
    probs = low(raised / lax.optimization_barrier(jnp.sum(raised, axis=-1, keepdims=True)))
    context = jnp.einsum('bhqk,bkhd->bqhd', probs, values, precision=HIGHEST).reshape(rows, D)
    context = low(low_back(context))
    attended = inputs + low_back(jnp.dot(context, w_out, precision=HIGHEST))
    hidden_two = low(layer_norm(attended, gain_two, shift_two))
    gate_pre = low_back(jnp.dot(hidden_two, w_gate, precision=HIGHEST))
    up_pre = low_back(jnp.dot(hidden_two, w_up, precision=HIGHEST))
    inner = low(gate_pre * jax.nn.sigmoid(gate_pre) * up_pre)
    return attended + low_back(jnp.dot(inner, w_down, precision=HIGHEST))

def reference(tokens, segment_ids, w_qkv, qv_bias, w_out, ln1_gain, ln1_bias, w_gate, w_up, w_down, ln2_gain, ln2_bias, out_grad):
    group_rows = MB * CAP
    groups = tokens.shape[0] // group_rows
    weights = tuple((array.astype(jnp.float32) for array in (w_qkv, qv_bias, w_out, ln1_gain, ln1_bias, w_gate, w_up, w_down, ln2_gain, ln2_bias)))
    stacked = (tokens.reshape(groups, group_rows, D), segment_ids.reshape(groups, MB, CAP), out_grad.reshape(groups, group_rows, D))

    def accumulate(running, element):
        group_tokens, group_segments, group_grad = element

        def layer(inputs, *params):
            return forward(inputs, group_segments, *params)
        output, puller = jax.vjp(layer, group_tokens.astype(jnp.float32), *weights)
        grads = puller(group_grad.astype(jnp.float32))
        running = tuple((left + right for left, right in zip(running, grads[1:])))
        return (running, (output.astype(jnp.bfloat16), grads[0].astype(jnp.bfloat16)))
    initial = tuple((jnp.zeros(weight.shape, jnp.float32) for weight in weights))
    totals, (outputs, input_grads) = lax.scan(accumulate, initial, stacked)
    return (outputs.reshape(-1, D), input_grads.reshape(-1, D)) + totals
```

```python
import jax
import jax.numpy as jnp
from jax import lax
from jax.sharding import PartitionSpec as P

D = 1024
H = 16
HD = 64
ROT = 16
CAP = 64
EPS = 1e-05
BF = jnp.bfloat16
F32 = jnp.float32

TB = 4
TG = 2 * TB
PAD = 16


def dot(left, right):
    return jnp.dot(left, right, preferred_element_type=F32)


def contract_rows(left, right):
    return lax.dot_general(left, right, (((0,), (0,)), ((), ())), preferred_element_type=F32)


def contract_cols(left, right):
    return lax.dot_general(left, right, (((1,), (1,)), ((), ())), preferred_element_type=F32)


def layer_stats(values):
    center = jnp.mean(values, axis=-1, keepdims=True)
    shifted = values - center
    inverse = lax.rsqrt(jnp.mean(shifted * shifted, axis=-1, keepdims=True) + EPS)
    return (shifted * inverse, inverse)


def norm_input_grad(grad_output, normed, inverse, gain):
    scaled = grad_output * gain
    return inverse * (
        scaled
        - jnp.mean(scaled, axis=-1, keepdims=True)
        - normed * jnp.mean(scaled * normed, axis=-1, keepdims=True)
    )


def slot_layout(segments):
    width = segments.shape[1]
    same = segments[:, :, None] == segments[:, None, :]
    order = jnp.arange(width)
    earlier = order[:, None] > order[None, :]
    positions = jnp.sum((same & earlier).astype(F32), axis=-1)
    allowed = same & (order[:, None] >= order[None, :])
    return (positions, allowed)


def rotary_tables(positions):
    freqs = 10000.0 ** (-2.0 * jnp.arange(ROT // 2, dtype=F32) / ROT)
    angles = positions[:, :, None, None] * freqs
    return (jnp.cos(angles), jnp.sin(angles))


def rotate(values, cosine, sine):
    half = ROT // 2
    first = values[..., :half]
    second = values[..., half:ROT]
    return jnp.concatenate(
        [first * cosine - second * sine, second * cosine + first * sine, values[..., ROT:]], axis=-1
    )


def unrotate(grads, cosine, sine):
    half = ROT // 2
    first = grads[..., :half]
    second = grads[..., half:ROT]
    return jnp.concatenate(
        [first * cosine + second * sine, second * cosine - first * sine, grads[..., ROT:]], axis=-1
    )


def attention_scores(queries, keys, allowed):
    scores = jnp.einsum("bqhd,bkhd->bhqk", queries, keys, preferred_element_type=F32) * 0.125
    return jnp.where(allowed[:, None], scores, -1e30)


def make_device_fn(fsdp):
    groups = fsdp // TB

    def across(x, flip):
        return lax.ppermute(x, "fsdp", [(i, i ^ flip) for i in range(fsdp)])

    def near(x, j):
        return x if j == 0 else across(x, j)

    def far(x, j):
        return x if j == 0 else across(x, j * TB)

    def pair(x):
        return lax.ppermute(x, "rep", [(0, 1), (1, 0)])

    def gather_rows(x):
        slots = []
        for j in range(TB):
            got = near(x, j)
            slots += [got, pair(got)]
        return slots

    def scatter_rows(parts):
        given = pair(jnp.stack([parts[2 * j + 1] for j in range(TB)]).astype(BF))
        sums = [parts[2 * j] + given[j].astype(F32) for j in range(TB)]
        total = sums[0]
        for j in range(1, TB):
            total = total + near(sums[j].astype(BF), j).astype(F32)
        return total

    def pick(x, i):
        return lax.dynamic_index_in_dim(x, i, 0, keepdims=False)

    def on_device(
        tokens,
        segment_ids,
        w_qkv,
        qv_bias,
        w_out,
        ln1_gain,
        ln1_bias,
        w_gate,
        w_up,
        w_down,
        ln2_gain,
        ln2_bias,
        out_grad,
    ):
        rows = tokens.shape[0]
        batches = segment_ids.shape[0] * TG
        dr = w_qkv.shape[0]
        width = D // TG
        ff = w_gate.shape[1]
        unit = ff // (fsdp * 2)
        me = lax.axis_index("fsdp")
        rep = lax.axis_index("rep")
        a, b = me // TB, me % TB
        t = 2 * b + rep
        all_rows = rows * TG

        ids = jnp.zeros((PAD, D), BF).at[0, :rows].set(segment_ids.reshape(rows).astype(BF))
        token_slots = gather_rows(jnp.concatenate([tokens, ids]))
        x_rows = jnp.concatenate([s[:rows] for s in token_slots])
        segments = jnp.stack([s[rows, :rows] for s in token_slots]).reshape(batches, CAP)

        small = jnp.concatenate([ln1_gain, ln1_bias, ln2_gain, ln2_bias, qv_bias])
        n_small = small.shape[0]
        qkv_blocks = w_qkv.reshape(dr, 3, TG, width).transpose(2, 0, 1, 3).reshape(TG, dr, 3 * width)
        row = jnp.zeros((PAD, 3 * width), BF).at[0, :n_small].set(small)
        qkv_blocks = jnp.concatenate([qkv_blocks, jnp.broadcast_to(row, (TG, PAD, 3 * width))], 1)
        got = jnp.stack([near(pick(qkv_blocks, 2 * (b ^ j) + rep), j) for j in range(TB)])
        got = jnp.stack([far(got, j) for j in range(groups)]).reshape(fsdp, dr + PAD, 3 * width)
        got = jnp.take(got, jnp.arange(fsdp) ^ me, axis=0)
        qkv = got[:, :dr].reshape(D, 3 * width)
        smalls = got[:, dr, :n_small].astype(F32)
        gain_one, shift_one, gain_two, shift_two = (
            smalls[:, i * dr : (i + 1) * dr].reshape(D) for i in range(4)
        )
        bias = smalls[:, 4 * dr :].reshape(2, TG, width)
        bias_row = jnp.concatenate([pick(bias[0], t), jnp.zeros((width,), F32), pick(bias[1], t)])

        half = w_out.reshape(2, dr // 2, D)
        got = pick(half, rep)
        got = jnp.stack([far(got, j) for j in range(groups)])
        got = jnp.stack([near(got, j) for j in range(TB)], axis=1)
        got = jnp.stack([got, pair(got)], axis=2)
        out_full = jnp.take(
            got.reshape(fsdp * 2, dr // 2, D), jnp.arange(fsdp * 2) ^ (2 * me + rep), axis=0
        ).reshape(D, D)

        def columns(w):
            w = w.reshape(dr, groups, TB, 2, unit).transpose(2, 3, 0, 1, 4)
            return w.reshape(TG, dr, groups * unit)

        feed = jnp.concatenate([columns(w_gate), columns(w_up)], axis=2)
        got = jnp.stack([near(pick(feed, 2 * (b ^ j) + rep), j) for j in range(TB)])
        got = jnp.stack([far(got, j) for j in range(groups)]).reshape(fsdp, dr, -1)
        feed = jnp.take(got, jnp.arange(fsdp) ^ me, axis=0).reshape(D, -1)
        units = groups * unit
        gate_w, up_w = feed[:, :units], feed[:, units:]
        got = pick(w_down.reshape(2, unit, D), rep)
        got = jnp.stack([far(got, j) for j in range(groups)])
        down_w = jnp.take(got, jnp.arange(groups) ^ a, axis=0).reshape(units, D)

        g_rows = jnp.concatenate(gather_rows(out_grad))

        inputs = x_rows.astype(F32)
        normed_one, inverse_one = layer_stats(inputs)
        hidden_one = (normed_one * gain_one + shift_one).astype(BF)
        projected = (dot(hidden_one, qkv) + bias_row).reshape(batches, CAP, 3, width // HD, HD)
        positions, allowed = slot_layout(segments)
        cosine, sine = rotary_tables(positions)
        queries = rotate(projected[:, :, 0], cosine, sine).astype(BF)
        keys = rotate(projected[:, :, 1], cosine, sine).astype(BF)
        values = projected[:, :, 2].astype(BF)
        scores = attention_scores(queries, keys, allowed)
        highest = jnp.max(scores, axis=-1, keepdims=True)
        raised = jnp.exp(scores - highest)
        totals = jnp.sum(raised, axis=-1, keepdims=True)
        log_total = highest + jnp.log(totals)
        probs = (raised / totals).astype(BF)
        context = jnp.einsum("bhqk,bkhd->bqhd", probs, values, preferred_element_type=F32)
        context = context.reshape(all_rows, width).astype(BF)

        slots = gather_rows(context)
        slots = [
            jnp.take(s.reshape(TG, rows, width), jnp.arange(TG) ^ j, axis=0).reshape(all_rows, width)
            for j, s in enumerate(slots)
        ]
        context_full = (
            jnp.take(jnp.stack(slots), jnp.arange(TG) ^ t, axis=0)
            .transpose(1, 0, 2)
            .reshape(all_rows, D)
        )
        attended = inputs + dot(context_full, out_full)
        normed_two, inverse_two = layer_stats(attended)
        hidden_two = (normed_two * gain_two + shift_two).astype(BF)
        gate_pre = dot(hidden_two, gate_w)
        up_pre = dot(hidden_two, up_w)
        sigmoid_gate = jax.nn.sigmoid(gate_pre)
        activated = gate_pre * sigmoid_gate
        inner = (activated * up_pre).astype(BF)

        grad_inner = contract_cols(g_rows, down_w)
        grad_gate = (
            grad_inner * up_pre * (sigmoid_gate * (1.0 + gate_pre * (1.0 - sigmoid_gate)))
        ).astype(BF)
        grad_up = (grad_inner * activated).astype(BF)
        partial = contract_cols(grad_gate, gate_w) + contract_cols(grad_up, up_w)
        grad_hidden_two = scatter_rows(list(partial.reshape(TG, rows, D)))
        own_normed, own_inverse = normed_two[:rows], inverse_two[:rows]
        grad_middle = out_grad.astype(F32) + norm_input_grad(
            grad_hidden_two, own_normed, own_inverse, gain_two
        )
        gain_two_grad = jnp.sum(grad_hidden_two * own_normed, axis=0)
        shift_two_grad = jnp.sum(grad_hidden_two, axis=0)

        result = scatter_rows(list(dot(inner, down_w).reshape(TG, rows, D)))
        result = (attended[:rows] + result).astype(BF)

        def settle_far(term):
            total = pick(term, a).astype(F32)
            for j in range(1, groups):
                total = total + far(pick(term, a ^ j), j).astype(F32)
            return total

        def settle(term):
            n, columns = term.shape[1:]
            total = settle_far(term.reshape(groups, TB, n, columns)).astype(BF)
            got = jnp.stack([near(pick(total, b ^ j), j) for j in range(TB)])
            got = jnp.stack([got, pair(got)], axis=1).reshape(TG, n, columns)
            return jnp.take(got, jnp.arange(TG) ^ t, axis=0)

        feed_term = jnp.concatenate(
            [contract_rows(hidden_two, grad_gate), contract_rows(hidden_two, grad_up)], axis=1
        ).astype(BF)
        feed_grad = settle(feed_term.reshape(fsdp, dr, 2 * units))

        def uncolumns(g):
            g = g.reshape(TB, 2, dr, groups, unit).transpose(2, 3, 0, 1, 4)
            return g.reshape(dr, ff).astype(F32)

        gate_grad = uncolumns(feed_grad[:, :, :units])
        up_grad = uncolumns(feed_grad[:, :, units:])
        down_term = contract_rows(inner, g_rows).astype(BF).reshape(groups, unit, D)
        got = settle_far(down_term).astype(BF)
        other = pair(got)
        down_grad = jnp.where(
            rep == 0, jnp.concatenate([got, other]), jnp.concatenate([other, got])
        ).astype(F32)

        grad_branch = grad_middle.astype(BF)
        grad_context = contract_cols(grad_branch, out_full).astype(BF)
        blocks = jnp.concatenate(
            [grad_context.reshape(rows, TG, width), grad_branch.reshape(rows, TG, width)], axis=2
        ).transpose(1, 0, 2)
        blocks = blocks.reshape(TB, 2, rows, 2 * width)
        mine = lax.dynamic_index_in_dim(blocks, rep, 1, keepdims=False)
        theirs = pair(lax.dynamic_index_in_dim(blocks, 1 - rep, 1, keepdims=False))
        both = jnp.stack([mine, theirs], axis=1)
        got = jnp.stack([near(pick(both, b ^ j), j) for j in range(TB)])
        got = got.reshape(all_rows, 2 * width)
        grad_context = got[:, :width].reshape(batches, CAP, width // HD, HD)
        branch_columns = got[:, width:]
        out_term = contract_rows(context_full, branch_columns)

        scores_again = attention_scores(queries, keys, allowed)
        probs_again = jnp.exp(scores_again - log_total)
        grad_values = jnp.einsum(
            "bhqk,bqhd->bkhd", probs_again.astype(BF), grad_context, preferred_element_type=F32
        )
        grad_probs = jnp.einsum(
            "bqhd,bkhd->bhqk", grad_context, values, preferred_element_type=F32
        )
        grad_scores = probs_again * (
            grad_probs - jnp.sum(probs_again * grad_probs, axis=-1, keepdims=True)
        )
        grad_scores = grad_scores.astype(BF)
        grad_queries = (
            jnp.einsum("bhqk,bkhd->bqhd", grad_scores, keys, preferred_element_type=F32) * 0.125
        )
        grad_keys = (
            jnp.einsum("bhqk,bqhd->bkhd", grad_scores, queries, preferred_element_type=F32) * 0.125
        )
        grad_projected = jnp.stack(
            [unrotate(grad_queries, cosine, sine), unrotate(grad_keys, cosine, sine), grad_values],
            axis=2,
        )
        grad_projected = grad_projected.reshape(all_rows, 3 * width).astype(BF)
        partial = contract_cols(grad_projected, qkv)
        gain_one_grad = jnp.sum(partial * normed_one, axis=0)
        shift_one_grad = jnp.sum(partial, axis=0)
        grad_hidden_one = scatter_rows(list(partial.reshape(TG, rows, D)))
        grad_tokens = (
            grad_middle
            + norm_input_grad(grad_hidden_one, normed_one[:rows], inverse_one[:rows], gain_one)
        ).astype(BF)

        qkv_term = contract_rows(hidden_one, grad_projected)
        column_sums = jnp.sum(grad_projected.astype(F32), axis=0)
        bias_term = jnp.zeros((2, TG, width), F32)
        bias_term = bias_term.at[0, t].set(column_sums[:width]).at[1, t].set(column_sums[2 * width :])
        smalls = [gain_one_grad, shift_one_grad, gain_two_grad, shift_two_grad, bias_term]
        smalls = jnp.concatenate([s.reshape(fsdp, -1) for s in smalls], axis=1)
        smalls = jnp.pad(smalls[:, None], ((0, 0), (0, PAD - 1), (0, 4 * width - n_small)))
        term = jnp.concatenate([qkv_term, out_term], axis=1).reshape(fsdp, dr, 4 * width)
        term = jnp.concatenate([term, smalls], axis=1).astype(BF)
        grads = settle(term)
        owned = jnp.sum(grads[:, dr, :n_small].astype(F32), axis=0)
        grads = grads[:, :dr].reshape(TG, dr, 4, width).transpose(1, 2, 0, 3).astype(F32)
        qkv_grad = grads[:, :3].reshape(dr, 3 * D)
        out_w_grad = grads[:, 3].reshape(dr, D)
        ln = [owned[i * dr : (i + 1) * dr] for i in range(4)]
        return (
            result,
            grad_tokens,
            qkv_grad,
            owned[4 * dr :],
            out_w_grad,
            ln[0],
            ln[1],
            gate_grad,
            up_grad,
            down_grad,
            ln[2],
            ln[3],
        )

    return on_device


def solution(mesh):
    weight, vector = P("fsdp", None), P("fsdp")
    rows = P(("fsdp", "rep"), None)
    return jax.shard_map(
        make_device_fn(mesh.shape["fsdp"]),
        mesh=mesh,
        in_specs=(rows, rows, weight, vector, weight, vector, vector)
        + (weight, weight, weight, vector, vector, rows),
        out_specs=(rows, rows, weight, vector, weight, vector, vector)
        + (weight, weight, weight, vector, vector),
        check_vma=False,
    )
```

```python
import functools

import jax
import jax.numpy as jnp
from jax import lax
from jax.experimental import pallas as pl
from jax.experimental.pallas import tpu as pltpu
from jax.sharding import PartitionSpec as P

D = 1024
HD = 64
ROT = 16
CAP = 64
EPS = 1e-05
BF = jnp.bfloat16
F32 = jnp.float32

TB = 4
TG = 2 * TB
W = D // TG
PAD = 16
ROWS = 128
ALL = TG * ROWS
STEP = 2 * ROWS


VM = pl.BlockSpec(memory_space=pltpu.VMEM)
SM = pl.BlockSpec(memory_space=pltpu.SMEM)


def nn(left, right):
    return jnp.dot(left, right, preferred_element_type=F32)


def tn(left, right):
    return lax.dot_general(left, right, (((0,), (0,)), ((), ())), preferred_element_type=F32)


def nt(left, right):
    return lax.dot_general(left, right, (((1,), (1,)), ((), ())), preferred_element_type=F32)


def call(body, name, n_in, outs, scratch=(), smem=True):
    specs = ([SM] if smem else []) + [VM] * n_in
    return pl.pallas_call(
        body,
        out_shape=[jax.ShapeDtypeStruct(s, d) for s, d in outs],
        in_specs=specs,
        out_specs=[VM] * len(outs),
        scratch_shapes=[pltpu.VMEM(s, d) for s, d in scratch],
        name=name,
    )


def place(idx):
    me, rep = idx[0], idx[1]
    a, b = me // TB, me % TB
    return me, rep, a, b, 2 * b + rep


def at(start, size, unit):
    return pl.ds(pl.multiple_of(start, unit), size)


def layer_stats(values):
    center = jnp.mean(values, axis=-1, keepdims=True)
    shifted = values - center
    inverse = lax.rsqrt(jnp.mean(shifted * shifted, axis=-1, keepdims=True) + EPS)
    return (shifted * inverse, inverse)


def norm_input_grad(grad_output, normed, inverse, gain):
    scaled = grad_output * gain
    return inverse * (
        scaled
        - jnp.mean(scaled, axis=-1, keepdims=True)
        - normed * jnp.mean(scaled * normed, axis=-1, keepdims=True)
    )


def iota(shape, dim):
    return lax.broadcasted_iota(jnp.int32, shape, dim)


def prepare_body(fsdp, dr, ff, idx, w_qkv, w_gate, w_up, w_out, small, seg, *refs):
    q_out, f_out, o_out, feed = refs[:TB], refs[TB : 2 * TB], refs[2 * TB], refs[2 * TB + 1]
    me, rep, a, b, t = place(idx)
    groups = fsdp // TB
    unit = ff // (2 * fsdp)
    nb = 2 * D // fsdp
    gains = small[...].astype(F32)
    spread = (iota((dr, D), 1) == me * dr + iota((dr, D), 0)).astype(F32)
    rows = []
    for i in range(4):
        full = nn(gains[:, i * dr : (i + 1) * dr], spread)
        last = jnp.concatenate([full[:, 6 * W :], jnp.zeros((1, W), F32)], 1)
        rows += [full[:, : 3 * W], full[:, 3 * W : 6 * W], last]
    bias = gains[:, 4 * dr : 4 * dr + nb]
    ids = seg[...].astype(F32)
    ids = jnp.concatenate([ids[0:1], ids[1:2], jnp.zeros((1, 2 * W), F32)], 1)
    lane = iota((nb, 3 * W), 1)
    source = me * nb + iota((nb, 3 * W), 0)
    for j in range(TB):
        to = 2 * (b ^ j) + rep
        for s in range(3):
            q_out[j][:dr, s * W : (s + 1) * W] = w_qkv[:, at(s * D + to * W, W, W)]
        wanted = jnp.where(lane < W, to * W + lane, D + to * W + lane - 2 * W)
        wanted = jnp.where((lane >= W) & (lane < 2 * W), -1, wanted)
        bias_row = nn(bias, (wanted == source).astype(F32))
        block = jnp.concatenate(rows + [bias_row, ids, jnp.zeros((2, 3 * W), F32)], 0)
        q_out[j][dr:, :] = block.astype(BF)
    o_out[...] = w_out[:, at(rep * (D // 2), D // 2, D // 2)]
    for near in range(TB):
        pieces = []
        for w in (w_gate, w_up):
            for far in range(groups):
                start = (far * TB + near) * 2 * unit
                both = w[:, start : start + 2 * unit].astype(F32)
                pieces.append(jnp.where(rep == 0, both[:, :unit], both[:, unit:]))
        feed[near] = jnp.concatenate(pieces, 1).astype(BF)
    for j in range(TB):
        f_out[j][...] = feed[b ^ j]


def stack_body(dr, *refs):
    slots, (out, ids) = refs[:TB], refs[TB:]
    smalls = jnp.zeros((PAD, 3 * W), F32)
    rows = []
    for j in range(TB):
        out[j * dr : (j + 1) * dr, :] = slots[j][:dr, :]
        block = slots[j][dr:, :].astype(F32)
        smalls = smalls + block
        rows.append(block[13:14, :W])
    out[TB * dr :, :] = smalls.astype(BF)
    ids[...] = jnp.concatenate(rows + [jnp.zeros((PAD - TB, W), F32)], 0).astype(BF)


def attend_body(fsdp, dr, idx, *refs):
    groups = fsdp // TB
    xs, far, (ids_own, ids_pair, table) = refs[:TG], refs[TG : TG + groups], refs[TG + groups : TG + groups + 3]
    context, x_out, hidden_out, qkv_out, probs_out, weight, tables, params, ids = refs[TG + groups + 3 :]
    me, rep, a, b, t = place(idx)
    smalls = jnp.zeros((PAD, 3 * W), F32)
    for i in range(groups):
        for j in range(TB):
            to = (a ^ i) * TB + (b ^ j)
            weight[at(to * dr, dr, dr), :] = far[i][j * dr : (j + 1) * dr, :]
        smalls = smalls + far[i][TB * dr :, :].astype(F32)
    gains = [
        jnp.concatenate(
            [smalls[3 * i : 3 * i + 1], smalls[3 * i + 1 : 3 * i + 2], smalls[3 * i + 2 : 3 * i + 3, : 2 * W]], 1
        )
        for i in range(4)
    ]
    params[...] = jnp.concatenate(gains + [jnp.zeros((4, D), F32)], 0)
    bias = smalls[12:13]
    for j in range(TB):
        ids[2 * j : 2 * j + 1, :] = ids_own[j : j + 1, :].astype(F32)
        ids[2 * j + 1 : 2 * j + 2, :] = ids_pair[j : j + 1, :].astype(F32)
    for i in range(TG):
        x_out[i * ROWS : (i + 1) * ROWS, :] = xs[i][...]

    row, col = iota((ROWS, ROWS), 0), iota((ROWS, ROWS), 1)
    apart = (row // CAP) != (col // CAP)
    heads = [(iota((1, W), 1) // HD == h).astype(F32).astype(BF) for h in range(W // HD)]

    def step(n, carry):
        block = at(n * STEP, STEP, STEP)
        normed, _ = layer_stats(x_out[block, :].astype(F32))
        hidden = (normed * params[0:1, :] + params[1:2, :]).astype(BF)
        hidden_out[block, :] = hidden
        projected = nn(hidden, weight[...]) + bias
        for k in range(2):
            part = at(n * STEP + k * ROWS, ROWS, ROWS)
            p = projected[k * ROWS : (k + 1) * ROWS]
            across = jnp.broadcast_to(ids[pl.ds(2 * n + k, 1), :], (ROWS, ROWS))
            same = (across == across.T) & jnp.logical_not(apart)
            position = jnp.sum((same & (row > col)).astype(F32), axis=-1, keepdims=True)
            allowed = same & (row >= col)
            chosen = (iota((ROWS, CAP), 1).astype(F32) == position).astype(F32)
            rot = jnp.dot(chosen, table[...], precision=lax.Precision.HIGHEST, preferred_element_type=F32)
            tables[part, :] = rot
            cosine, left, right = rot[:, :W], rot[:, W : 2 * W], rot[:, 2 * W :]

            def turn(v):
                return v * cosine + pltpu.roll(v, W - ROT // 2, 1) * left + pltpu.roll(v, ROT // 2, 1) * right

            q, key, value = turn(p[:, :W]).astype(BF), turn(p[:, W : 2 * W]).astype(BF), p[:, 2 * W :].astype(BF)
            qkv_out[part, :W] = q
            qkv_out[part, W : 2 * W] = key
            qkv_out[part, 2 * W :] = value
            total = jnp.zeros((ROWS, W), F32)
            for h, head in enumerate(heads):
                scores = jnp.where(allowed, nt(q * head, key) * 0.125, -1e30)
                raised = jnp.exp(scores - jnp.max(scores, axis=-1, keepdims=True))
                probs = raised / jnp.sum(raised, axis=-1, keepdims=True)
                probs_out[(2 * n + k) * len(heads) + h] = probs
                total = total + nn(probs.astype(BF), value * head)
            context[part, :] = total.astype(BF)
        return carry

    lax.fori_loop(0, ALL // STEP, step, 0)


def feed_body(fsdp, dr, ff, idx, *refs):
    groups = fsdp // TB
    units = ff // TG
    refs = list(refs)

    def take(n):
        got = refs[:n]
        del refs[:n]
        return got

    contexts, outs, gs, far = take(TG), take(TG), take(TG), take(groups)
    x_rows, down, params = take(3)
    to_pair, own, attended_own, hidden_out, gate_out, up_out, inner_out, g_rows, context, out_full = take(10)
    gate_w, up_w = refs
    me, rep, a, b, t = place(idx)
    for j in range(TG):
        for p in range(TG):
            q = p ^ j
            context[p * ROWS : (p + 1) * ROWS, at((t ^ j) * W, W, W)] = contexts[j][q * ROWS : (q + 1) * ROWS, :]
        g_rows[j * ROWS : (j + 1) * ROWS, :] = gs[j][...]
    for j in range(TB):
        for k in range(2):
            for i in range(groups):
                to = (a ^ i) * TB + (b ^ j)
                out_full[at(to * dr, dr, dr), at((rep ^ k) * (D // 2), D // 2, D // 2)] = outs[2 * j + k][
                    i * dr : (i + 1) * dr, :
                ]
    for i in range(groups):
        for j in range(TB):
            to = at(((a ^ i) * TB + (b ^ j)) * dr, dr, dr)
            both = far[i][j * dr : (j + 1) * dr, :].astype(F32)
            gate_w[to, :] = both[:, :units].astype(BF)
            up_w[to, :] = both[:, units:].astype(BF)

    def step(n, carry):
        block = at(n * STEP, STEP, STEP)
        attended = x_rows[block, :].astype(F32) + nn(context[block, :], out_full[...])

        @pl.when(n == 0)
        def _():
            attended_own[...] = attended[:ROWS]

        normed, _ = layer_stats(attended)
        hidden = (normed * params[2:3, :] + params[3:4, :]).astype(BF)
        hidden_out[block, :] = hidden
        gate = nn(hidden, gate_w[...])
        up = nn(hidden, up_w[...])
        s = jax.nn.sigmoid(gate)
        activated = gate * s
        inner_out[block, :] = (activated * up).astype(BF)
        grad_inner = nt(g_rows[block, :], down[...])
        grad_gate = (grad_inner * up * (s * (1.0 + gate * (1.0 - s)))).astype(BF)
        grad_up = (grad_inner * activated).astype(BF)
        gate_out[block, :] = grad_gate
        up_out[block, :] = grad_up
        partial = nt(grad_gate, gate_w[...]) + nt(grad_up, up_w[...])
        own[n] = partial[:ROWS]
        to_pair[n] = partial[ROWS:].astype(BF)
        return carry

    lax.fori_loop(0, ALL // STEP, step, 0)


def result_body(inner, down, to_pair, own):
    def step(n, carry):
        partial = nn(inner[at(n * STEP, STEP, STEP), :], down[...])
        own[n] = partial[:ROWS]
        to_pair[n] = partial[ROWS:].astype(BF)
        return carry

    lax.fori_loop(0, ALL // STEP, step, 0)


def feed_grad_body(fsdp, dr, ff, idx, hidden, grad_gate, grad_up, inner, g_rows, *refs):
    groups = fsdp // TB
    units = ff // TG
    out, down_term, term = refs[:groups], refs[groups], refs[groups + 1]
    me, rep, a, b, t = place(idx)

    def step(n, carry):
        block = at(n * STEP, STEP, STEP)
        h = hidden[:, block]
        term[block, :] = jnp.concatenate([tn(h, grad_gate[...]), tn(h, grad_up[...])], 1).astype(BF)
        down_term[:, block] = tn(inner[...], g_rows[:, block]).astype(BF)
        return carry

    lax.fori_loop(0, D // STEP, step, 0)
    for i in range(groups):
        out[i][...] = term[at((a ^ i) * TB * dr, TB * dr, dr), :]


def combine_body(own, given, *refs):
    for j in range(TB):
        total = own[j] + given[j].astype(F32)
        refs[j][...] = total if j == 0 else total.astype(BF)


def middle_body(idx, own, r1, r2, r3, g, attended, out_full, params, middle, mine, theirs, sums):
    me, rep, a, b, t = place(idx)
    grad_hidden = own[...] + r1[...].astype(F32) + r2[...].astype(F32) + r3[...].astype(F32)
    normed, inverse = layer_stats(attended[...])
    grad = g[...].astype(F32) + norm_input_grad(grad_hidden, normed, inverse, params[2:3, :])
    middle[...] = grad
    gain_grad = jnp.sum(grad_hidden * normed, axis=0, keepdims=True)
    shift_grad = jnp.sum(grad_hidden, axis=0, keepdims=True)
    sums[...] = jnp.concatenate([gain_grad, shift_grad, jnp.zeros((6, D), F32)], 0)
    branch = grad.astype(BF)
    for j in range(TB):
        for k, out in ((0, mine), (1, theirs)):
            to = 2 * (b ^ j) + (rep ^ k)
            rows = out_full[at(to * W, W, W), :]
            out[j, :, :W] = nt(branch, rows).astype(BF)
    for to in range(TG):
        part = branch[:, to * W : (to + 1) * W]
        flip = t ^ to

        @pl.when(flip % 2 == 0)
        def _():
            mine[flip // 2, :, W:] = part

        @pl.when(flip % 2 == 1)
        def _():
            theirs[flip // 2, :, W:] = part


def attend_grad_body(fsdp, dr, idx, *refs):
    groups = fsdp // TB
    got = refs[:TB]
    qkv, probs, x_rows, hidden, weight, context, params, tables, sums = refs[TB : TB + 9]
    to_pair, own = refs[TB + 9 : TB + 11]
    out = refs[TB + 11 : TB + 11 + groups]
    grads, branch, term, vectors = refs[TB + 11 + groups :]
    me, rep, a, b, t = place(idx)
    heads = [(iota((1, W), 1) // HD == h).astype(F32).astype(BF) for h in range(W // HD)]
    for j in range(TB):
        for k in range(2):
            branch[(2 * j + k) * ROWS : (2 * j + k + 1) * ROWS, :] = got[j][k, :, :]
    vectors[...] = jnp.zeros((8, D), F32)
    vectors[2:4, :] = sums[0:2, :]

    def step(n, carry):
        gain_grad, shift_grad, q_sum, v_sum = carry
        block = at(n * STEP, STEP, STEP)
        for k in range(2):
            part = at(n * STEP + k * ROWS, ROWS, ROWS)
            q, key, value = qkv[part, :W], qkv[part, W : 2 * W], qkv[part, 2 * W :]
            gc = branch[part, :W]
            rot = tables[part, :]
            cosine, left, right = rot[:, :W], rot[:, W : 2 * W], rot[:, 2 * W :]
            gq = jnp.zeros((ROWS, W), F32)
            gk = jnp.zeros((ROWS, W), F32)
            gv = jnp.zeros((ROWS, W), F32)
            for h, head in enumerate(heads):
                p = probs[(2 * n + k) * len(heads) + h]
                gch = gc * head
                gv = gv + tn(p.astype(BF), gch)
                gp = nt(gch, value)
                gs = (p * (gp - jnp.sum(p * gp, axis=-1, keepdims=True))).astype(BF)
                gq = gq + nn(gs, key * head)
                gk = gk + tn(gs, q * head)

            def back(v):
                return v * cosine - pltpu.roll(v, W - ROT // 2, 1) * left - pltpu.roll(v, ROT // 2, 1) * right

            gq = back(gq * 0.125).astype(BF)
            gk = back(gk * 0.125).astype(BF)
            gv = gv.astype(BF)
            grads[part, :W] = gq
            grads[part, W : 2 * W] = gk
            grads[part, 2 * W :] = gv
            q_sum = q_sum + jnp.sum(gq.astype(F32), axis=0, keepdims=True)
            v_sum = v_sum + jnp.sum(gv.astype(F32), axis=0, keepdims=True)
        partial = nt(grads[block, :], weight[...])
        normed, _ = layer_stats(x_rows[block, :].astype(F32))
        gain_grad = gain_grad + jnp.sum(partial * normed, axis=0, keepdims=True)
        shift_grad = shift_grad + jnp.sum(partial, axis=0, keepdims=True)
        own[n] = partial[:ROWS]
        to_pair[n] = partial[ROWS:].astype(BF)
        return gain_grad, shift_grad, q_sum, v_sum

    zero, zero_w = jnp.zeros((1, D), F32), jnp.zeros((1, W), F32)
    gain_grad, shift_grad, q_sum, v_sum = lax.fori_loop(0, ALL // STEP, step, (zero, zero, zero_w, zero_w))
    vectors[0:1, :] = gain_grad
    vectors[1:2, :] = shift_grad
    vectors[4:5, at(t * W, W, W)] = q_sum
    vectors[5:6, at(t * W, W, W)] = v_sum

    def weights(n, carry):
        block = at(n * STEP, STEP, STEP)
        term[block, : 3 * W] = tn(hidden[:, block], grads[...]).astype(BF)
        term[block, 3 * W :] = tn(context[:, block], branch[:, W:]).astype(BF)
        return carry

    lax.fori_loop(0, D // STEP, weights, 0)
    every = vectors[...]
    smalls = [every[i : i + 1, h * 4 * W : (h + 1) * 4 * W] for i in range(6) for h in range(2)]
    smalls = jnp.concatenate(smalls + [jnp.zeros((4, 4 * W), F32)], 0).astype(BF)
    for i in range(groups):
        out[i][: TB * dr, :] = term[at((a ^ i) * TB * dr, TB * dr, dr), :]
        out[i][TB * dr :, :] = smalls


def tokens_body(own, r1, r2, r3, tokens, middle, params, out):
    grad_hidden = own[...] + r1[...].astype(F32) + r2[...].astype(F32) + r3[...].astype(F32)
    normed, inverse = layer_stats(tokens[...].astype(F32))
    grad = middle[...] + norm_input_grad(grad_hidden, normed, inverse, params[0:1, :])
    out[...] = grad.astype(BF)


def far_sum_body(groups, dr, extra, idx, *refs):
    parts, out = refs[:groups], refs[groups:]
    me, rep, a, b, t = place(idx)
    for j in range(TB):
        rows = at((b ^ j) * dr, dr, dr)
        total = parts[0][rows, :].astype(F32)
        for part in parts[1:]:
            total = total + part[rows, :].astype(F32)
        out[j][:dr, :] = total.astype(BF)
    if extra:
        total = parts[0][TB * dr :, :].astype(F32)
        for part in parts[1:]:
            total = total + part[TB * dr :, :].astype(F32)
        for j in range(TB):
            out[j][dr:, :] = total.astype(BF)


def attend_final_body(fsdp, dr, idx, *refs):
    slots, (qkv_grad, out_grad, smalls, ln) = refs[:TG], refs[TG : TG + 4]
    me, rep, a, b, t = place(idx)
    total = jnp.zeros((PAD, 4 * W), F32)
    for j in range(TB):
        for k in range(2):
            slot = slots[2 * j + k]
            to = 2 * (b ^ j) + (rep ^ k)
            for s in range(3):
                qkv_grad[:, at(s * D + to * W, W, W)] = slot[:dr, s * W : (s + 1) * W].astype(F32)
            out_grad[:, at(to * W, W, W)] = slot[:dr, 3 * W :].astype(F32)
            total = total + slot[dr:, :].astype(F32)
    smalls[...] = total
    ln[...] = jnp.zeros((8, W), F32)


def feed_final_body(fsdp, dr, ff, idx, *refs):
    slots, (gate_grad, up_grad, blocks) = refs[:TG], refs[TG:]
    me, rep, a, b, t = place(idx)
    groups = fsdp // TB
    unit = ff // (2 * fsdp)
    for j in range(TB):
        for k in range(2):
            blocks[2 * (b ^ j) + (rep ^ k)] = slots[2 * j + k][...].astype(F32)
    for w, out in enumerate((gate_grad, up_grad)):
        pieces = []
        for far in range(groups):
            for t2 in range(TG):
                start = (w * groups + far) * unit
                pieces.append(blocks[t2, :, start : start + unit])
        out[...] = jnp.concatenate(pieces, 1)


def make_device_fn(fsdp):
    groups = fsdp // TB

    def across(x, flip):
        return lax.ppermute(x, "fsdp", [(i, i ^ flip) for i in range(fsdp)])

    def near(x, j):
        return x if j == 0 else across(x, j)

    def far(x, j):
        return x if j == 0 else across(x, j * TB)

    def pair(x):
        return lax.ppermute(x, "rep", [(0, 1), (1, 0)])

    def gather_rows(x):
        slots = []
        for j in range(TB):
            got = near(x, j)
            slots += [got, pair(got)]
        return slots

    def scatter_rows(own, to_pair):
        parts = call(
            combine_body, "combine", 2, [((ROWS, D), F32)] + [((ROWS, D), BF)] * (TB - 1), smem=False
        )(own, pair(to_pair))
        return [near(part, j) for j, part in enumerate(parts)]

    def pick(x, i):
        return lax.dynamic_index_in_dim(x, i, 0, keepdims=False)

    def on_device(
        tokens,
        segment_ids,
        w_qkv,
        qv_bias,
        w_out,
        ln1_gain,
        ln1_bias,
        w_gate,
        w_up,
        w_down,
        ln2_gain,
        ln2_bias,
        out_grad,
    ):
        dr = w_qkv.shape[0]
        ff = w_gate.shape[1]
        unit = ff // (fsdp * 2)
        units = groups * unit
        me = lax.axis_index("fsdp")
        rep = lax.axis_index("rep")
        a, b = me // TB, me % TB
        idx = jnp.where(jnp.arange(2) == 0, me, rep).astype(jnp.int32)

        xs = gather_rows(tokens)

        small = jnp.concatenate([ln1_gain, ln1_bias, ln2_gain, ln2_bias, qv_bias])
        prepared = call(
            functools.partial(prepare_body, fsdp, dr, ff),
            "prepare",
            6,
            [((dr + PAD, 3 * W), BF)] * TB + [((dr, 2 * units), BF)] * TB + [((dr, D // 2), BF)],
            [((TB, dr, 2 * units), BF)],
        )(idx, w_qkv, w_gate, w_up, w_out, small[None], segment_ids)
        q_msgs, f_msgs, out_half = prepared[:TB], prepared[TB : 2 * TB], prepared[2 * TB]

        q_slots = [near(m, j) for j, m in enumerate(q_msgs)]
        q_far, ids_own = call(
            functools.partial(stack_body, dr),
            "stack",
            TB,
            [((TB * dr + PAD, 3 * W), BF), ((PAD, W), BF)],
            smem=False,
        )(*q_slots)
        ids_pair = pair(ids_own)
        q_far = [far(q_far, j) for j in range(groups)]

        f_far = jnp.concatenate([near(m, j) for j, m in enumerate(f_msgs)], 0)
        f_far = [far(f_far, j) for j in range(groups)]
        got = pick(w_down.reshape(2, unit, D), rep)
        got = jnp.stack([far(got, j) for j in range(groups)])
        down = jnp.take(got, jnp.arange(groups) ^ a, axis=0).reshape(units, D)
        got = jnp.concatenate([far(out_half, j) for j in range(groups)], 0)
        outs = gather_rows(got)
        gs = gather_rows(out_grad)

        freqs = 10000.0 ** (-2.0 * jnp.arange(ROT // 2, dtype=F32) / ROT)
        angles = jnp.arange(CAP, dtype=F32)[:, None] * freqs
        cosine, sine = jnp.cos(angles), jnp.sin(angles)
        one, zero, none = jnp.ones((CAP, HD - ROT)), jnp.zeros((CAP, HD - ROT // 2)), jnp.zeros((CAP, ROT // 2))
        heads = W // HD
        table = jnp.concatenate(
            [cosine, cosine, one] * heads + [-sine, zero] * heads + [none, sine, zero[:, ROT // 2 :]] * heads, 1
        ).astype(F32)

        context, x_rows, hidden_one, qkv, probs, qkv_w, tables, params, _ = call(
            functools.partial(attend_body, fsdp, dr),
            "attend",
            TG + groups + 3,
            [
                ((ALL, W), BF),
                ((ALL, D), BF),
                ((ALL, D), BF),
                ((ALL, 3 * W), BF),
                ((TG * heads, ROWS, ROWS), F32),
                ((D, 3 * W), BF),
                ((ALL, 3 * W), F32),
                ((8, D), F32),
                ((TG, W), F32),
            ],
        )(idx, *xs, *q_far, ids_own, ids_pair, table)

        contexts = gather_rows(context)
        (
            to_pair,
            own,
            attended,
            hidden_two,
            grad_gate,
            grad_up,
            inner,
            g_rows,
            context_full,
            out_full,
        ) = call(
            functools.partial(feed_body, fsdp, dr, ff),
            "feed",
            3 * TG + groups + 3,
            [
                ((TB, ROWS, D), BF),
                ((TB, ROWS, D), F32),
                ((ROWS, D), F32),
                ((ALL, D), BF),
                ((ALL, units), BF),
                ((ALL, units), BF),
                ((ALL, units), BF),
                ((ALL, D), BF),
                ((ALL, D), BF),
                ((D, D), BF),
            ],
            [((D, units), BF), ((D, units), BF)],
        )(idx, *contexts, *outs, *gs, *f_far, x_rows, down, params)

        parts = scatter_rows(own, to_pair)
        middle, mine, theirs, sums = call(
            middle_body,
            "middle",
            8,
            [((ROWS, D), F32), ((TB, ROWS, 2 * W), BF), ((TB, ROWS, 2 * W), BF), ((8, D), F32)],
        )(idx, *parts, out_grad, attended, out_full, params)

        feed_terms = call(
            functools.partial(feed_grad_body, fsdp, dr, ff),
            "feed_grad",
            5,
            [((TB * dr, 2 * units), BF)] * groups + [((units, D), BF)],
            [((D, 2 * units), BF)],
        )(idx, hidden_two, grad_gate, grad_up, inner, g_rows)
        feed_terms, down_term = feed_terms[:groups], feed_terms[groups]

        to_pair, own = call(
            result_body, "result", 2, [((TB, ROWS, D), BF), ((TB, ROWS, D), F32)], smem=False
        )(inner, down)
        r = scatter_rows(own, to_pair)
        result = (attended + r[0] + r[1].astype(F32) + r[2].astype(F32) + r[3].astype(F32)).astype(BF)

        def settle(terms, extra):
            n, columns = terms[0].shape
            got = [far(term, j) for j, term in enumerate(terms)]
            msgs = call(
                functools.partial(far_sum_body, groups, dr, extra),
                "far_sum",
                groups,
                [((dr + extra, columns), BF)] * TB,
            )(idx, *got)
            got = [near(m, j) for j, m in enumerate(msgs)]
            return [s for g in got for s in (g, pair(g))]

        slots = settle(feed_terms, 0)
        gate_grad, up_grad = call(
            functools.partial(feed_final_body, fsdp, dr, ff),
            "feed_final",
            TG,
            [((dr, ff), F32)] * 2,
            [((TG, dr, 2 * units), F32)],
        )(idx, *slots)
        down_term = down_term.reshape(groups, unit, D)
        got = pick(down_term, a).astype(F32)
        for j in range(1, groups):
            got = got + far(pick(down_term, a ^ j), j).astype(F32)
        got = got.astype(BF)
        other = pair(got)
        down_grad = jnp.where(
            rep == 0, jnp.concatenate([got, other]), jnp.concatenate([other, got])
        ).astype(F32)

        theirs = pair(theirs)
        both = [jnp.stack([mine[j], theirs[j]]) for j in range(TB)]
        got = [near(m, j) for j, m in enumerate(both)]
        att = call(
            functools.partial(attend_grad_body, fsdp, dr),
            "attend_grad",
            TB + 9,
            [((TB, ROWS, D), BF), ((TB, ROWS, D), F32)] + [((TB * dr + PAD, 4 * W), BF)] * groups,
            [((ALL, 3 * W), BF), ((ALL, 2 * W), BF), ((D, 4 * W), BF), ((8, D), F32)],
        )(idx, *got, qkv, probs, x_rows, hidden_one, qkv_w, context_full, params, tables, sums)
        to_pair, own, terms = att[0], att[1], att[2:]
        slots = settle(terms, PAD)
        parts = scatter_rows(own, to_pair)
        (grad_tokens,) = call(tokens_body, "tokens", 7, [((ROWS, D), BF)], smem=False)(
            *parts, tokens, middle, params
        )
        qkv_grad, out_w_grad, smalls, _ = call(
            functools.partial(attend_final_body, fsdp, dr),
            "attend_final",
            TG,
            [((dr, 3 * D), F32), ((dr, D), F32), ((PAD, 4 * W), F32), ((8, W), F32)],
        )(idx, *slots)
        smalls = smalls[:12].reshape(6, D)
        ln = lax.dynamic_slice(smalls, (0, me * dr), (4, dr))
        nb = 2 * D // fsdp
        bias_grad = lax.dynamic_slice(smalls[4:].reshape(2 * D), (me * nb,), (nb,))
        return (
            result,
            grad_tokens,
            qkv_grad,
            bias_grad,
            out_w_grad,
            ln[0],
            ln[1],
            gate_grad,
            up_grad,
            down_grad,
            ln[2],
            ln[3],
        )

    return on_device


def solution(mesh):
    weight, vector = P("fsdp", None), P("fsdp")
    rows = P(("fsdp", "rep"), None)
    return jax.shard_map(
        make_device_fn(mesh.shape["fsdp"]),
        mesh=mesh,
        in_specs=(rows, rows, weight, vector, weight, vector, vector)
        + (weight, weight, weight, vector, vector, rows),
        out_specs=(rows, rows, weight, vector, weight, vector, vector)
        + (weight, weight, weight, vector, vector),
        check_vma=False,
    )
```
